32 devices in a mesh: section: 4 (over x, core), obs: 8 (over z, y).
Axes of the slice: x: 2, y: 2, z: 4, core: 2. Of those that a mesh axis runs over, the one named last changes fastest.
Arguments:
- predictors: bfloat16 [4, 4, 20, 32768], P('section', None, None, 'obs'), may hold values from -5 to 5
- departures: float32 [4, 4, 32768], P('section', None, 'obs'), may hold values from -30 to 30
- obs_precision: float32 [4, 4, 32768], P('section', None, 'obs'), may hold values from 0.3 to 3
- qc_pass: int32 [4, 4, 32768], P('section', None, 'obs'), may hold values 0 or 1
- block_channel: int32 [4, 4, 256], P('section', None, 'obs'), may hold values from 0 to 2047, as said below
- stream_order: int32 [4], replicated, may hold values from 0 to 3, each once
- prior_coeffs: float32 [4, 20, 2048], P(None, None, 'obs'), may hold values from -1 to 1
- prior_info: float32 [4, 210, 2048], P(None, None, 'obs'), may hold values from -1 to 32, as said below
- memory_factor: float32 [2048], P('obs'), may hold values from 0.5 to 0.98
Outputs:
- coeffs: float32 [4, 4, 20, 2048], P('section', None, None, 'obs')
- information: float32 [4, 4, 210, 2048], P('section', None, None, 'obs')
The draws below stay inside these ranges and needn't reach their ends.
Inputs may be any that keep to these rules, and one draw needn't show every extreme that they name: `block_channel`: among the 32 row blocks of one index of obs, at most 8 have channels in any one range of the 256 channels from a multiple of 256; in every window and stream one such range holds exactly 8 blocks of every index of obs. `stream_order`: each stream appears once. `prior_info`: for every stream and channel the 210 entries are the upper triangle, row by row, of a symmetric positive definite matrix of order 20.
All inputs are finite; a program needn't handle non-finite values. No bound on the sum of `qc_pass` on one device may be relied on, other than what follows from the above.
Results may differ from the reference program's by a relative error of at most 0.0038.
Values sent between devices are 32-bit elements; how exact they have to be, the bound alone decides.
A program may use at most 64 MiB of HBM per device.

```python
import math
import jax
import jax.numpy as jnp
import numpy as np
from jax import lax

NPRED = 20
CH = 2048
BLOCK_ROWS = 128
STREAMS = 4
WINDOWS = 4
ROWS = 32768
NB_DEV = 32
NBLK = 256
CH_DEV = 256
CAP = 8


def observation_fields(base_key):
    pred_key, truth_key, noise_key = jax.random.split(jax.random.fold_in(base_key, 11), 3)
    values = jax.random.truncated_normal(pred_key, -5.0, 5.0, (WINDOWS, STREAMS, NPRED, ROWS), jnp.float32)
    true_coeffs = 0.25 * jax.random.truncated_normal(truth_key, -4.0, 4.0, (WINDOWS, STREAMS, NPRED, NBLK), jnp.float32)
    signal = jnp.einsum('wspbr,wspb->wsbr', values.reshape(WINDOWS, STREAMS, NPRED, NBLK, BLOCK_ROWS), true_coeffs).reshape(WINDOWS, STREAMS, ROWS)
    position = jnp.arange(ROWS, dtype=jnp.float32) / ROWS
    spread = 1.0 + 2.0 * position
    noise_draw = jax.random.truncated_normal(noise_key, -5.0, 5.0, (WINDOWS, STREAMS, ROWS), jnp.float32)
    return (values, jnp.clip(signal + spread * noise_draw, -30.0, 30.0))


def draw_predictors(key, part):
    return observation_fields(key)[0].astype(jnp.bfloat16)


def draw_departures(key, part):
    return observation_fields(key)[1]


def draw_block_channel(key, part):
    owner_count = NBLK // NB_DEV

    def one_group(group_key):
        pick_key, device_key = jax.random.split(group_key)
        special = jax.random.randint(pick_key, (), 0, owner_count)

        def one_device(own_key):
            list_key, shuffle_key, inner_key = jax.random.split(own_key, 3)
            others = jax.random.permutation(list_key, (owner_count - 1) * CAP)[:NB_DEV - CAP]
            other_owner = (others // CAP + special + 1) % owner_count
            owners = jnp.concatenate([jnp.full((CAP,), special, jnp.int32), other_owner.astype(jnp.int32)])
            owners = jax.random.permutation(shuffle_key, owners)
            inner_channel = jax.random.randint(inner_key, (NB_DEV,), 0, CH_DEV)
            return (owners * CH_DEV + inner_channel).astype(jnp.int32)
        return jax.vmap(one_device)(jax.random.split(device_key, owner_count)).reshape(NBLK)
    groups = jax.vmap(one_group)(jax.random.split(jax.random.fold_in(key, 31), WINDOWS * STREAMS))
    return groups.reshape(WINDOWS, STREAMS, NBLK)


def draw_prior_info(key, part):
    raw_key, margin_key = jax.random.split(jax.random.fold_in(key, 23))
    raw = jax.random.uniform(raw_key, (STREAMS, CH, NPRED, NPRED), jnp.float32, -1.0, 1.0)
    identity = jnp.eye(NPRED, dtype=jnp.float32)
    coupling = 0.5 * (raw + jnp.swapaxes(raw, 2, 3)) * (1.0 - identity)
    margin = jnp.exp(jax.random.uniform(margin_key, (STREAMS, CH, NPRED), jnp.float32, math.log(2.0), math.log(12.0)))
    leading = jnp.sum(jnp.abs(coupling), axis=3) + margin
    matrix = coupling + leading[..., None] * identity
    upper_index = np.array([i * NPRED + j for i in range(NPRED) for j in range(i, NPRED)], dtype=np.int32)
    packed = matrix.reshape(STREAMS, CH, NPRED * NPRED)[:, :, upper_index]
    return jnp.swapaxes(packed, 1, 2)


def place_ends(drawn, key, smallest, top_value):
    longest = drawn.shape.index(max(drawn.shape))
    spots = []
    for shift in (0, 1):
        where = [jax.random.randint(jax.random.fold_in(key, axis), (), 0, length) for axis, length in enumerate(drawn.shape)]
        where[longest] = (where[longest] + shift) % drawn.shape[longest]
        spots.append(tuple(where))
    return drawn.at[spots[0]].set(smallest).at[spots[1]].set(top_value)


def levels(stream_key, dims, pieces, least, top_value):
    factor_of = 1.0
    for axis_at, parts in pieces:
        heights = jax.random.uniform(jax.random.fold_in(jax.random.fold_in(stream_key, 6), axis_at), (parts,), jnp.float32, least / len(pieces), top_value / len(pieces))
        factor_of = factor_of * jnp.repeat(jnp.exp(heights), dims[axis_at] // parts).reshape((-1,) + (1,) * (len(dims) - 1 - axis_at))
    return factor_of


def scatter_about(key, extent, scale, reach, cuts=(), held_as=jnp.bfloat16):
    drawn = scale * jax.random.normal(key, extent, jnp.float32)
    if cuts:
        drawn = drawn * levels(key, extent, cuts, -0.22, 0.18)
    return jnp.clip(drawn, -reach, reach).astype(held_as)


def setup_inputs(seed: int = 0) -> dict:
    splits = jax.random.split(jax.random.key(seed), 10)
    predictors = draw_predictors(jax.random.fold_in(splits[9], 71), 0)
    departures = draw_departures(jax.random.fold_in(splits[9], 71), 0)
    obs_precision = jnp.clip(jnp.exp(math.log(3.0) - 2.3025851 * jax.random.uniform(splits[2], (WINDOWS, STREAMS, ROWS), jnp.float32) ** levels(splits[2], (WINDOWS, STREAMS, ROWS), ((0, 4), (2, 8)), -0.2, 0.2)), 0.3, 3.0)
    qc_pass = place_ends((jax.random.randint(splits[3], (WINDOWS, STREAMS, ROWS), 0, 4) < 3).astype(jnp.int32), jax.random.fold_in(splits[3], 1), 0, 1)
    block_channel = draw_block_channel(jax.random.fold_in(splits[9], 71), 0)
    stream_order = jax.random.permutation(splits[5], STREAMS).astype(jnp.int32)
    prior_coeffs = scatter_about(splits[6], (STREAMS, NPRED, CH), 0.25, 1.0, ((2, 8),), jnp.float32)
    prior_info = draw_prior_info(jax.random.fold_in(splits[9], 71), 0)
    memory_factor = jnp.clip(jnp.exp(math.log(0.98) - 0.6729445 * jax.random.uniform(splits[8], (CH,), jnp.float32) ** levels(splits[8], (CH,), ((0, 8),), -0.2, 0.2)), 0.5, 0.98)
    return {"predictors": predictors, "departures": departures, "obs_precision": obs_precision, "qc_pass": qc_pass, "block_channel": block_channel, "stream_order": stream_order, "prior_coeffs": prior_coeffs, "prior_info": prior_info, "memory_factor": memory_factor}


HUBER_SQ = 9.0
PRIOR_WEIGHT = 64.0

def upper_positions(dimension):
    return np.array([i * dimension + j for i in range(dimension) for j in range(i, dimension)], dtype=np.int32)

def solve_packed(packed, target):
    dimension = target.shape[0]
    placing = {}
    counter = 0
    for i in range(dimension):
        for j in range(i, dimension):
            placing[i, j] = counter
            counter += 1
    factor = [[None] * dimension for i in range(dimension)]
    for j in range(dimension):
        pivot_root = jnp.sqrt(packed[placing[j, j]] - sum((factor[j][k] * factor[j][k] for k in range(j))))
        factor[j][j] = pivot_root
        for i in range(j + 1, dimension):
            factor[i][j] = (packed[placing[j, i]] - sum((factor[i][k] * factor[j][k] for k in range(j)))) / pivot_root
    forward = []
    for i in range(dimension):
        forward.append((target[i] - sum((factor[i][k] * forward[k] for k in range(i)))) / factor[i][i])
    backward = [None] * dimension
    for i in reversed(range(dimension)):
        backward[i] = (forward[i] - sum((factor[k][i] * backward[k] for k in range(i + 1, dimension)))) / factor[i][i]
    return jnp.stack(backward)

def stream_update(beta_prior, info_prior, predicted, departed, precision, passed, channel):
    pred_count = predicted.shape[0]
    block_count = channel.shape[0]
    block_width = departed.shape[0] // block_count
    shaped = predicted.astype(jnp.float32).reshape(pred_count, block_count, block_width)
    block_coeffs = jnp.take(beta_prior, channel, axis=1)
    offset = lax.optimization_barrier(jnp.sum(shaped * block_coeffs[:, :, None], axis=0))
    residual = departed.reshape(block_count, block_width) - offset
    scale_row = precision.reshape(block_count, block_width)
    weight = passed.reshape(block_count, block_width).astype(jnp.float32) * scale_row / (1.0 + scale_row * residual * residual / HUBER_SQ)
    weighted = lax.optimization_barrier((weight[None] * shaped).astype(jnp.bfloat16)).astype(jnp.float32)
    chi_square = jnp.sum(weight * residual * residual)
    passed_count = jnp.sum(passed.astype(jnp.float32))
    inflation = (chi_square + PRIOR_WEIGHT) / (passed_count + PRIOR_WEIGHT)
    gram_upper = jnp.einsum('ibr,jbr->bij', weighted, shaped).reshape(block_count, pred_count * pred_count)[:, upper_positions(pred_count)]
    gradient = jnp.einsum('ibr,br->bi', weighted, residual)
    block_sums = jnp.concatenate([gram_upper, gradient], axis=1)
    normal = jax.ops.segment_sum(block_sums, channel, num_segments=CH).T
    tri_count = gram_upper.shape[1]
    info_post = info_prior + normal[:tri_count] / inflation
    beta_post = beta_prior + solve_packed(info_post, normal[tri_count:] / inflation)
    return (beta_post, info_post)

def reference(predictors, departures, obs_precision, qc_pass, block_channel, stream_order, prior_coeffs, prior_info, memory_factor):

    def window_step(state_pair, window):
        beta_prior, info_prior = state_pair

        def select_window(source):
            return jnp.take(lax.dynamic_index_in_dim(source, window, 0, keepdims=False), stream_order, axis=0)
        beta_post, info_post = jax.vmap(stream_update)(beta_prior, info_prior, select_window(predictors), select_window(departures), select_window(obs_precision), select_window(qc_pass), select_window(block_channel))
        return ((beta_post, memory_factor[None, None, :] * info_post), (beta_post, info_post))
    initial = (jnp.take(prior_coeffs, stream_order, axis=0), jnp.take(prior_info, stream_order, axis=0))
    final_state, outputs = lax.scan(window_step, initial, jnp.arange(WINDOWS, dtype=jnp.int32))
    return (outputs[0], outputs[1])
```

```python
import functools

import jax
import jax.numpy as jnp
import numpy as np
from jax import lax
from jax.experimental import pallas as pl
from jax.experimental.pallas import tpu as pltpu
from jax.sharding import PartitionSpec as P

HUBER_SQ = 9.0
PRIOR_WEIGHT = 64.0
F32 = jnp.float32
BF16 = jnp.bfloat16
NN = (((1,), (0,)), ((), ()))
NT = (((1,), (1,)), ((), ()))
TN = (((0,), (0,)), ((), ()))


def round_up(n, m):
    return -(-n // m) * m


def split3(x):
    hi = x.astype(BF16)
    rest = x - hi.astype(F32)
    mid = rest.astype(BF16)
    low = (rest - mid.astype(F32)).astype(BF16)
    return hi, mid, low


def dot(a, b, dims):
    return lax.dot_general(a, b, dims, preferred_element_type=F32)


def kernel(
    cfg,
    order_ref,
    x_ref,
    dep_ref,
    prec_ref,
    qc_ref,
    bc_ref,
    pc_ref,
    pi_ref,
    mf_ref,
    expand_ref,
    pick_ref,
    prefix_ref,
    co_ref,
    io_ref,
    xs,
    bcs,
    bcr,
    cs,
    cr,
    ts,
    tr,
    beta,
    state,
    work,
    info_out,
    beta_out,
    bc_send,
    bc_recv,
    c_send,
    c_recv,
    t_send,
    t_recv,
    o_send,
    o_recv,
):
    S, O, K, N, NP, T, C, NB, SL, TL = cfg
    sec = lax.axis_index("section")
    ob = lax.axis_index("obs")
    owner = sec < K
    mine = jnp.minimum(sec, K - 1)

    def send(src, dst, send_sem, recv_sem, s, o):
        here = (s == sec) & (o == ob)

        @pl.when(jnp.logical_not(here))
        def _():
            pltpu.make_async_remote_copy(
                src_ref=src,
                dst_ref=dst,
                send_sem=send_sem,
                recv_sem=recv_sem,
                device_id={"section": s, "obs": o},
                device_id_type=pl.DeviceIdType.MESH,
            ).start()

        @pl.when(here)
        def _():
            pltpu.make_async_copy(src, dst, recv_sem).start()

    def sent(src, send_sem, s, o):
        @pl.when(jnp.logical_not((s == sec) & (o == ob)))
        def _():
            pltpu.make_async_copy(src, src, send_sem).wait()

    def got(dst, recv_sem):
        pltpu.make_async_copy(dst, dst, recv_sem).wait()

    for k in range(K):
        bcs[k] = jnp.broadcast_to(bc_ref[order_ref[k]], (SL, 128))

    def send_channels(k, _):
        def one(o, _):
            send(bcs.at[k], bcr.at[sec, ob], bc_send.at[k, o], bc_recv.at[sec, ob], k, o)
            return 0

        return lax.fori_loop(0, O, one, 0)

    lax.fori_loop(0, K, send_channels, 0)

    for k in range(K):
        xs[k, 0:N, :] = x_ref[order_ref[k]].astype(F32)
        xs[k, N:NP, :] = jnp.zeros((NP - N, xs.shape[2]), F32)
    beta[...] = jnp.zeros_like(beta)
    beta[0:N, :] = pc_ref[order_ref[mine]]
    state[...] = pi_ref[order_ref[mine]]

    rows8 = lax.broadcasted_iota(jnp.int32, (O * SL, 128), 0)
    rank_of_row = (rows8 % SL + 1).astype(F32)

    def slots(channel, low):
        inside = (channel >= low) & (channel < low + C)
        rank = dot(jnp.where(inside, 1.0, 0.0).astype(BF16), prefix_ref[...], NN)
        return inside & (rank == rank_of_row)

    @pl.when(owner)
    def _():
        def arrive(w, _):
            def one(o, _):
                got(bcr.at[w, o], bc_recv.at[w, o])
                return 0

            return lax.fori_loop(0, O, one, 0)

        lax.fori_loop(0, S, arrive, 0)

    def row_entry(k, w):
        m = order_ref[k]
        placing = slots(
            jnp.broadcast_to(bc_ref[m], (O * SL, 128)), (rows8 // SL) * C
        )
        placing = jnp.where(placing, 1.0, 0.0).astype(BF16)

        def one(o, _):
            got(cr.at[k, o], c_recv.at[k, o])
            return 0

        lax.fori_loop(0, O, one, 0)
        parts = split3(cr[k].reshape(O * SL, 128))
        coef3 = jnp.concatenate(
            [dot(placing, part, TN)[0:NB, 0:NP] for part in parts], axis=0
        ).astype(BF16)
        sub = lax.broadcasted_iota(jnp.int32, (8, 128), 0)
        tiles = [jnp.zeros((8, 128), F32) for _ in range(NB // 8)]
        blocks = []
        for b in range(NB):
            xb = xs[k, :, b * 128 : (b + 1) * 128]
            xh = xb.astype(BF16)
            blocks.append(xb)
            full = dot(coef3, xh, NN)
            q = b // 8 * 8
            tile = full[q : q + 8] + full[NB + q : NB + q + 8] + full[2 * NB + q : 2 * NB + q + 8]
            tiles[b // 8] = jnp.where(sub == b % 8, tile, tiles[b // 8])
        offset = jnp.concatenate(tiles, axis=0)
        residual = dep_ref[m] - offset
        precision = prec_ref[m]
        passed = qc_ref[m].astype(F32)
        weight = passed * precision / (1.0 + precision * residual * residual / HUBER_SQ)
        total = jnp.sum(jnp.sum(weight * residual * residual, axis=0, keepdims=True), axis=1, keepdims=True)
        count = jnp.sum(jnp.sum(passed, axis=0, keepdims=True), axis=1, keepdims=True)
        pieces = [p.astype(F32) for p in split3(residual)]
        line = lax.broadcasted_iota(jnp.int32, (NP, 128), 0)
        grams = []
        for b in range(NB):
            xb = blocks[b]
            left = (weight[b : b + 1] * xb).astype(BF16)
            right = xb
            for p in range(3):
                right = jnp.where(line == N + p, pieces[p][b : b + 1], right)
            grams.append(dot(left, right.astype(BF16), NT))
        gram = jnp.concatenate(grams, axis=0)
        spread = sum(dot(part, expand_ref[...], NN) for part in split3(gram))
        packed = jnp.sum(spread.reshape(NB, NP, TL) * pick_ref[...][None], axis=1)
        out = sum(dot(placing[:, 0:NB], part, NN) for part in split3(packed))
        lane = lax.broadcasted_iota(jnp.int32, (O * SL, TL), 1)
        out = jnp.where(lane == T + N, total, jnp.where(lane == T + N + 1, count, out))
        ts[k] = out.reshape(O, SL, TL)

        def push(o, _):
            send(ts.at[k, o], tr.at[w, ob], t_send.at[k, o], t_recv.at[w, ob], k, o)
            return 0

        lax.fori_loop(0, O, push, 0)

    def owner_slots(w):
        channel = bcr[w].reshape(O * SL, 128)
        low = ob * C
        hit = slots(channel, low)
        value = jnp.sum(jnp.where(hit, (channel - low + 1).astype(F32), 0.0), axis=1, keepdims=True)
        lane = lax.broadcasted_iota(jnp.int32, (O * SL, C), 1).astype(F32)
        return jnp.where(lane == value - 1.0, 1.0, 0.0).astype(BF16)

    def solve(w):
        hot = owner_slots(w)

        def one(o, _):
            got(tr.at[w, o], t_recv.at[w, o])
            return 0

        lax.fori_loop(0, O, one, 0)
        terms = tr[w].reshape(O * SL, TL)
        row = lax.broadcasted_iota(jnp.int32, (O * SL, TL), 0)
        sums = jnp.sum(jnp.where(row % SL == 0, terms, 0.0), axis=0, keepdims=True)
        inverse = (sums[:, T + N + 1 : T + N + 2] + PRIOR_WEIGHT) / (sums[:, T + N : T + N + 1] + PRIOR_WEIGHT)
        normal = sum(dot(part, hot, TN) for part in split3(terms)) * inverse
        post = state[...] + normal[0:T]
        work[0:T, :] = post
        work[T:TL, :] = normal[T:TL]
        info_out[w] = post
        state[...] = post * mf_ref[...]
        send(info_out.at[w], io_ref.at[sec], o_send.at[w, 0], o_recv.at[sec, 0], w, ob)
        cols = []
        for k in range(N):
            at = k * N - k * (k - 1) // 2 - k
            cols.append(work[at : at + NP, :])
        target = work[T : T + NP, :]
        scales, forward, starts = [], [], [0] * N
        for j in range(N):
            scale = lax.rsqrt(cols[j][j - starts[j] : j - starts[j] + 1])
            scales.append(scale)
            base = j // 8 * 8
            factor = cols[j][base - starts[j] :] * scale
            cols[j] = factor
            starts[j] = base
            step = target[j : j + 1] * scale
            forward.append(step)
            target = target - jnp.concatenate([jnp.zeros((base, C), F32), factor * step], axis=0) if base else target - factor * step
            for k in range(j + 1, N):
                kb = k // 8 * 8
                cols[k] = cols[k][kb - starts[k] :] - factor[kb - base :] * factor[k - base : k - base + 1]
                starts[k] = kb
        index = lax.broadcasted_iota(jnp.int32, (NP, C), 0)
        answer = jnp.zeros((NP, C), F32)
        for i in reversed(range(N)):
            base = i // 8 * 8
            dots = jnp.sum(cols[i] * answer[base:], axis=0, keepdims=True)
            value = (forward[i] - dots) * scales[i]
            answer = jnp.where(index == i, value, answer)
        fresh = beta[0:N, :] + answer[0:N]
        beta[0:N, :] = fresh
        beta_out[w] = fresh
        send(beta_out.at[w], co_ref.at[sec], o_send.at[w, 1], o_recv.at[sec, 1], w, ob)

    def window(w, _):
        @pl.when(owner)
        def _():
            hot = owner_slots(w)
            cs[w] = sum(dot(hot, part, NT) for part in split3(beta[...])).reshape(O, SL, 128)

            def one(o, _):
                send(cs.at[w, o], cr.at[sec, ob], c_send.at[w, o], c_recv.at[sec, ob], w, o)
                return 0

            lax.fori_loop(0, O, one, 0)

        @pl.when(sec == w)
        def _():
            def entry(i, _):
                row_entry((w + 1 + i) % K, w)
                return 0

            lax.fori_loop(0, K, entry, 0)

        @pl.when(owner)
        def _():
            solve(w)

        return 0

    lax.fori_loop(0, S, window, 0)

    for k in range(K):
        got(io_ref.at[k], o_recv.at[k, 0])
        got(co_ref.at[k], o_recv.at[k, 1])

    def drain_rows(k, _):
        def one(o, _):
            sent(bcs.at[k], bc_send.at[k, o], k, o)
            sent(ts.at[k, o], t_send.at[k, o], k, o)
            return 0

        return lax.fori_loop(0, O, one, 0)

    lax.fori_loop(0, K, drain_rows, 0)

    @pl.when(owner)
    def _():
        def drain(w, _):
            def one(o, _):
                sent(cs.at[w, o], c_send.at[w, o], w, o)
                return 0

            lax.fori_loop(0, O, one, 0)
            sent(info_out.at[w], o_send.at[w, 0], w, ob)
            sent(beta_out.at[w], o_send.at[w, 1], w, ob)
            return 0

        lax.fori_loop(0, S, drain, 0)


def local(
    predictors,
    departures,
    obs_precision,
    qc_pass,
    block_channel,
    stream_order,
    prior_coeffs,
    prior_info,
    memory_factor,
):
    S, O = lax.axis_size("section"), lax.axis_size("obs")
    K, N, C = prior_coeffs.shape
    T = prior_info.shape[1]
    NB = block_channel.shape[2]
    R = predictors.shape[3]
    width = R // NB
    assert width == 128 and K <= S and NB <= 128 and NB % 8 == 0
    NP = round_up(N + 3, 8)
    SL = round_up(max(2 * NB // O, 1), 8)
    TL = round_up(T + N + 4, 128)
    pairs = [(i, j) for i in range(N) for j in range(i, N)]
    expand = np.zeros((NP, TL), np.float32)
    pick = np.zeros((NP, TL), np.float32)
    for t, (i, j) in enumerate(pairs):
        expand[j, t] = 1.0
        pick[i, t] = 1.0
    for i in range(N):
        expand[N : N + 3, T + i] = 1.0
        pick[i, T + i] = 1.0
    prefix = (np.arange(128)[:, None] <= np.arange(128)[None, :]).astype(np.float32)
    cfg = (S, O, K, N, NP, T, C, NB, SL, TL)
    channel = jnp.pad(block_channel[0], ((0, 0), (0, 128 - NB)), constant_values=-1)
    vm = pl.BlockSpec(memory_space=pltpu.VMEM)
    dma = pltpu.SemaphoreType.DMA
    coeffs, info = pl.pallas_call(
        functools.partial(kernel, cfg),
        out_shape=(
            jax.ShapeDtypeStruct((K, N, C), F32),
            jax.ShapeDtypeStruct((K, T, C), F32),
        ),
        in_specs=[pl.BlockSpec(memory_space=pltpu.SMEM)] + [vm] * 11,
        out_specs=(vm, vm),
        scratch_shapes=[
            pltpu.VMEM((K, NP, R), F32),
            pltpu.VMEM((K, SL, 128), jnp.int32),
            pltpu.VMEM((S, O, SL, 128), jnp.int32),
            pltpu.VMEM((S, O, SL, 128), F32),
            pltpu.VMEM((K, O, SL, 128), F32),
            pltpu.VMEM((K, O, SL, TL), F32),
            pltpu.VMEM((S, O, SL, TL), F32),
            pltpu.VMEM((128, C), F32),
            pltpu.VMEM((T, C), F32),
            pltpu.VMEM((TL, C), F32),
            pltpu.VMEM((S, T, C), F32),
            pltpu.VMEM((S, N, C), F32),
            dma((K, O)),
            dma((S, O)),
            dma((S, O)),
            dma((K, O)),
            dma((K, O)),
            dma((S, O)),
            dma((S, 2)),
            dma((K, 2)),
        ],
        compiler_params=pltpu.CompilerParams(
            has_side_effects=True, vmem_limit_bytes=60 * 1024 * 1024
        ),
    )(
        stream_order,
        predictors[0],
        departures[0].reshape(K, NB, width),
        obs_precision[0].reshape(K, NB, width),
        qc_pass[0].reshape(K, NB, width),
        channel.reshape(K, 1, 128),
        prior_coeffs,
        prior_info,
        memory_factor[None],
        jnp.asarray(expand, BF16),
        jnp.asarray(pick, F32),
        jnp.asarray(prefix, BF16),
    )
    return coeffs[None], info[None]


def solution(mesh):
    in_specs = (
        P("section", None, None, "obs"),
        P("section", None, "obs"),
        P("section", None, "obs"),
        P("section", None, "obs"),
        P("section", None, "obs"),
        P(),
        P(None, None, "obs"),
        P(None, None, "obs"),
        P("obs"),
    )
    out_specs = (P("section", None, None, "obs"), P("section", None, None, "obs"))
    return jax.shard_map(local, mesh=mesh, in_specs=in_specs, out_specs=out_specs, check_vma=False)
```

```python
import functools

import jax
import jax.numpy as jnp
import numpy as np
from jax import lax
from jax.experimental import pallas as pl
from jax.experimental.pallas import tpu as pltpu
from jax.sharding import PartitionSpec as P

HUBER_SQ = 9.0
PRIOR_WEIGHT = 64.0
F32 = jnp.float32
BF16 = jnp.bfloat16
NN = (((1,), (0,)), ((), ()))
NT = (((1,), (1,)), ((), ()))
TN = (((0,), (0,)), ((), ()))


def round_up(n, m):
    return -(-n // m) * m


def split3(x):
    hi = x.astype(BF16)
    rest = x - hi.astype(F32)
    mid = rest.astype(BF16)
    low = (rest - mid.astype(F32)).astype(BF16)
    return hi, mid, low


def dot(a, b, dims):
    return lax.dot_general(a, b, dims, preferred_element_type=F32)


def kernel(
    cfg,
    order_ref,
    x_ref,
    dep_ref,
    prec_ref,
    qc_ref,
    bc_ref,
    pc_ref,
    pi_ref,
    mf_ref,
    expand_ref,
    pick_ref,
    prefix_ref,
    co_ref,
    io_ref,
    xs,
    bcs,
    bcr,
    cs,
    cr,
    ts,
    tr,
    beta,
    state,
    work,
    info_out,
    beta_out,
    bc_send,
    bc_recv,
    c_send,
    c_recv,
    t_send,
    t_recv,
    o_send,
    o_recv,
):
    S, O, K, N, NP, T, C, NB, SL, TL = cfg
    sec = lax.axis_index("section")
    ob = lax.axis_index("obs")
    owner = sec < K
    mine = jnp.minimum(sec, K - 1)

    def send(src, dst, send_sem, recv_sem, s, o):
        here = (s == sec) & (o == ob)

        @pl.when(jnp.logical_not(here))
        def _():
            pltpu.make_async_remote_copy(
                src_ref=src,
                dst_ref=dst,
                send_sem=send_sem,
                recv_sem=recv_sem,
                device_id={"section": s, "obs": o},
                device_id_type=pl.DeviceIdType.MESH,
            ).start()

        @pl.when(here)
        def _():
            pltpu.make_async_copy(src, dst, recv_sem).start()

    def sent(src, send_sem, s, o):
        @pl.when(jnp.logical_not((s == sec) & (o == ob)))
        def _():
            pltpu.make_async_copy(src, src, send_sem).wait()

    def got(dst, recv_sem):
        pltpu.make_async_copy(dst, dst, recv_sem).wait()

    for k in range(K):
        bcs[k] = jnp.broadcast_to(bc_ref[order_ref[k]], (SL, 128))

    def send_channels(k, _):
        def one(o, _):
            send(bcs.at[k], bcr.at[sec, ob], bc_send.at[k, o], bc_recv.at[sec, ob], k, o)
            return 0

        return lax.fori_loop(0, O, one, 0)

    lax.fori_loop(0, K, send_channels, 0)

    for k in range(K):
        xs[k, 0:N, :] = x_ref[order_ref[k]].astype(F32)
        xs[k, N:NP, :] = jnp.zeros((NP - N, xs.shape[2]), F32)
    beta[...] = jnp.zeros_like(beta)
    beta[0:N, :] = pc_ref[order_ref[mine]]
    state[...] = pi_ref[order_ref[mine]]

    rows8 = lax.broadcasted_iota(jnp.int32, (O * SL, 128), 0)
    rank_of_row = (rows8 % SL + 1).astype(F32)

    def slots(channel, low):
        inside = (channel >= low) & (channel < low + C)
        rank = dot(jnp.where(inside, 1.0, 0.0).astype(BF16), prefix_ref[...], NN)
        return inside & (rank == rank_of_row)

    @pl.when(owner)
    def _():
        def arrive(w, _):
            def one(o, _):
                got(bcr.at[w, o], bc_recv.at[w, o])
                return 0

            return lax.fori_loop(0, O, one, 0)

        lax.fori_loop(0, S, arrive, 0)

    def row_entry(k, w):
        m = order_ref[k]
        placing = slots(
            jnp.broadcast_to(bc_ref[m], (O * SL, 128)), (rows8 // SL) * C
        )
        placing = jnp.where(placing, 1.0, 0.0).astype(BF16)

        def one(o, _):
            got(cr.at[k, o], c_recv.at[k, o])
            return 0

        lax.fori_loop(0, O, one, 0)
        parts = split3(cr[k].reshape(O * SL, 128))
        coef3 = jnp.concatenate(
            [dot(placing, part, TN)[0:NB, 0:NP] for part in parts], axis=0
        ).astype(BF16)
        sub = lax.broadcasted_iota(jnp.int32, (8, 128), 0)
        tiles = [jnp.zeros((8, 128), F32) for _ in range(NB // 8)]
        blocks = []
        for b in range(NB):
            xb = xs[k, :, b * 128 : (b + 1) * 128]
            xh = xb.astype(BF16)
            blocks.append(xb)
            full = dot(coef3, xh, NN)
            q = b // 8 * 8
            tile = full[q : q + 8] + full[NB + q : NB + q + 8] + full[2 * NB + q : 2 * NB + q + 8]
            tiles[b // 8] = jnp.where(sub == b % 8, tile, tiles[b // 8])
        offset = jnp.concatenate(tiles, axis=0)
        residual = dep_ref[m] - offset
        precision = prec_ref[m]
        passed = qc_ref[m].astype(F32)
        weight = passed * precision / (1.0 + precision * residual * residual / HUBER_SQ)
        total = jnp.sum(jnp.sum(weight * residual * residual, axis=0, keepdims=True), axis=1, keepdims=True)
        count = jnp.sum(jnp.sum(passed, axis=0, keepdims=True), axis=1, keepdims=True)
        pieces = [p.astype(F32) for p in split3(residual)]
        line = lax.broadcasted_iota(jnp.int32, (NP, 128), 0)
        grams = []
        for b in range(NB):
            xb = blocks[b]
            left = (weight[b : b + 1] * xb).astype(BF16)
            right = xb
            for p in range(3):
                right = jnp.where(line == N + p, pieces[p][b : b + 1], right)
            grams.append(dot(left, right.astype(BF16), NT))
        gram = jnp.concatenate(grams, axis=0)
        spread = sum(dot(part, expand_ref[...], NN) for part in split3(gram))
        packed = jnp.sum(spread.reshape(NB, NP, TL) * pick_ref[...][None], axis=1)
        out = sum(dot(placing[:, 0:NB], part, NN) for part in split3(packed))
        lane = lax.broadcasted_iota(jnp.int32, (O * SL, TL), 1)
        out = jnp.where(lane == T + N, total, jnp.where(lane == T + N + 1, count, out))
        ts[k] = out.reshape(O, SL, TL)

        def push(o, _):
            send(ts.at[k, o], tr.at[w, ob], t_send.at[k, o], t_recv.at[w, ob], k, o)
            return 0

        lax.fori_loop(0, O, push, 0)

    def owner_slots(w):
        channel = bcr[w].reshape(O * SL, 128)
        low = ob * C
        hit = slots(channel, low)
        value = jnp.sum(jnp.where(hit, (channel - low + 1).astype(F32), 0.0), axis=1, keepdims=True)
        lane = lax.broadcasted_iota(jnp.int32, (O * SL, C), 1).astype(F32)
        return jnp.where(lane == value - 1.0, 1.0, 0.0).astype(BF16)

    def send_info(w):
        send(info_out.at[w], io_ref.at[sec], o_send.at[w, 0], o_recv.at[sec, 0], w, ob)

    def solve(w):
        hot = owner_slots(w)

        def one(o, _):
            got(tr.at[w, o], t_recv.at[w, o])
            return 0

        lax.fori_loop(0, O, one, 0)
        terms = tr[w].reshape(O * SL, TL)
        row = lax.broadcasted_iota(jnp.int32, (O * SL, TL), 0)
        sums = jnp.sum(jnp.where(row % SL == 0, terms, 0.0), axis=0, keepdims=True)
        inverse = (sums[:, T + N + 1 : T + N + 2] + PRIOR_WEIGHT) / (sums[:, T + N : T + N + 1] + PRIOR_WEIGHT)
        normal = sum(dot(part, hot, TN) for part in split3(terms)) * inverse
        post = state[...] + normal[0:T]
        work[0:T, :] = post
        work[T:TL, :] = normal[T:TL]
        info_out[w] = post
        state[...] = post * mf_ref[...]

        @pl.when(w == S - 1)
        def _():
            send_info(w)

        cols = []
        for k in range(N):
            at = k * N - k * (k - 1) // 2 - k
            cols.append(work[at : at + NP, :])
        target = work[T : T + NP, :]
        scales, forward, starts = [], [], [0] * N
        for j in range(N):
            scale = lax.rsqrt(cols[j][j - starts[j] : j - starts[j] + 1])
            scales.append(scale)
            base = j // 8 * 8
            factor = cols[j][base - starts[j] :] * scale
            cols[j] = factor
            starts[j] = base
            step = target[j : j + 1] * scale
            forward.append(step)
            target = target - jnp.concatenate([jnp.zeros((base, C), F32), factor * step], axis=0) if base else target - factor * step
            for k in range(j + 1, N):
                kb = k // 8 * 8
                cols[k] = cols[k][kb - starts[k] :] - factor[kb - base :] * factor[k - base : k - base + 1]
                starts[k] = kb
        index = lax.broadcasted_iota(jnp.int32, (NP, C), 0)
        answer = jnp.zeros((NP, C), F32)
        for i in reversed(range(N)):
            base = i // 8 * 8
            dots = jnp.sum(cols[i] * answer[base:], axis=0, keepdims=True)
            value = (forward[i] - dots) * scales[i]
            answer = jnp.where(index == i, value, answer)
        fresh = beta[0:N, :] + answer[0:N]
        beta[0:N, :] = fresh
        beta_out[w] = fresh
        send(beta_out.at[w], co_ref.at[sec], o_send.at[w, 1], o_recv.at[sec, 1], w, ob)

    def window(w, _):
        @pl.when(owner)
        def _():
            hot = owner_slots(w)
            cs[w] = sum(dot(hot, part, NT) for part in split3(beta[...])).reshape(O, SL, 128)

            def one(o, _):
                send(cs.at[w, o], cr.at[sec, ob], c_send.at[w, o], c_recv.at[sec, ob], w, o)
                return 0

            lax.fori_loop(0, O, one, 0)

        @pl.when(sec == w)
        def _():
            def entry(i, _):
                row_entry((w + 1 + i) % K, w)
                return 0

            lax.fori_loop(0, K, entry, 0)

        @pl.when(owner & (w > 0))
        def _():
            send_info(w - 1)

        @pl.when(owner)
        def _():
            solve(w)

        return 0

    lax.fori_loop(0, S, window, 0)

    for k in range(K):
        got(io_ref.at[k], o_recv.at[k, 0])
        got(co_ref.at[k], o_recv.at[k, 1])

    def drain_rows(k, _):
        def one(o, _):
            sent(bcs.at[k], bc_send.at[k, o], k, o)
            sent(ts.at[k, o], t_send.at[k, o], k, o)
            return 0

        return lax.fori_loop(0, O, one, 0)

    lax.fori_loop(0, K, drain_rows, 0)

    @pl.when(owner)
    def _():
        def drain(w, _):
            def one(o, _):
                sent(cs.at[w, o], c_send.at[w, o], w, o)
                return 0

            lax.fori_loop(0, O, one, 0)
            sent(info_out.at[w], o_send.at[w, 0], w, ob)
            sent(beta_out.at[w], o_send.at[w, 1], w, ob)
            return 0

        lax.fori_loop(0, S, drain, 0)


def local(
    predictors,
    departures,
    obs_precision,
    qc_pass,
    block_channel,
    stream_order,
    prior_coeffs,
    prior_info,
    memory_factor,
):
    S, O = lax.axis_size("section"), lax.axis_size("obs")
    K, N, C = prior_coeffs.shape
    T = prior_info.shape[1]
    NB = block_channel.shape[2]
    R = predictors.shape[3]
    width = R // NB
    assert width == 128 and K <= S and NB <= 128 and NB % 8 == 0
    NP = round_up(N + 3, 8)
    SL = round_up(max(2 * NB // O, 1), 8)
    TL = round_up(T + N + 4, 128)
    pairs = [(i, j) for i in range(N) for j in range(i, N)]
    expand = np.zeros((NP, TL), np.float32)
    pick = np.zeros((NP, TL), np.float32)
    for t, (i, j) in enumerate(pairs):
        expand[j, t] = 1.0
        pick[i, t] = 1.0
    for i in range(N):
        expand[N : N + 3, T + i] = 1.0
        pick[i, T + i] = 1.0
    prefix = (np.arange(128)[:, None] <= np.arange(128)[None, :]).astype(np.float32)
    cfg = (S, O, K, N, NP, T, C, NB, SL, TL)
    channel = jnp.pad(block_channel[0], ((0, 0), (0, 128 - NB)), constant_values=-1)
    vm = pl.BlockSpec(memory_space=pltpu.VMEM)
    dma = pltpu.SemaphoreType.DMA
    coeffs, info = pl.pallas_call(
        functools.partial(kernel, cfg),
        out_shape=(
            jax.ShapeDtypeStruct((K, N, C), F32),
            jax.ShapeDtypeStruct((K, T, C), F32),
        ),
        in_specs=[pl.BlockSpec(memory_space=pltpu.SMEM)] + [vm] * 11,
        out_specs=(vm, vm),
        scratch_shapes=[
            pltpu.VMEM((K, NP, R), F32),
            pltpu.VMEM((K, SL, 128), jnp.int32),
            pltpu.VMEM((S, O, SL, 128), jnp.int32),
            pltpu.VMEM((S, O, SL, 128), F32),
            pltpu.VMEM((K, O, SL, 128), F32),
            pltpu.VMEM((K, O, SL, TL), F32),
            pltpu.VMEM((S, O, SL, TL), F32),
            pltpu.VMEM((128, C), F32),
            pltpu.VMEM((T, C), F32),
            pltpu.VMEM((TL, C), F32),
            pltpu.VMEM((S, T, C), F32),
            pltpu.VMEM((S, N, C), F32),
            dma((K, O)),
            dma((S, O)),
            dma((S, O)),
            dma((K, O)),
            dma((K, O)),
            dma((S, O)),
            dma((S, 2)),
            dma((K, 2)),
        ],
        compiler_params=pltpu.CompilerParams(
            has_side_effects=True, vmem_limit_bytes=60 * 1024 * 1024
        ),
    )(
        stream_order,
        predictors[0],
        departures[0].reshape(K, NB, width),
        obs_precision[0].reshape(K, NB, width),
        qc_pass[0].reshape(K, NB, width),
        channel.reshape(K, 1, 128),
        prior_coeffs,
        prior_info,
        memory_factor[None],
        jnp.asarray(expand, BF16),
        jnp.asarray(pick, F32),
        jnp.asarray(prefix, BF16),
    )
    return coeffs[None], info[None]


def solution(mesh):
    in_specs = (
        P("section", None, None, "obs"),
        P("section", None, "obs"),
        P("section", None, "obs"),
        P("section", None, "obs"),
        P("section", None, "obs"),
        P(),
        P(None, None, "obs"),
        P(None, None, "obs"),
        P("obs"),
    )
    out_specs = (P("section", None, None, "obs"), P("section", None, None, "obs"))
    return jax.shard_map(local, mesh=mesh, in_specs=in_specs, out_specs=out_specs, check_vma=False)
```

```python
import functools

import jax
import jax.numpy as jnp
import numpy as np
from jax import lax
from jax.experimental import pallas as pl
from jax.experimental.pallas import tpu as pltpu
from jax.sharding import PartitionSpec as P

HUBER_SQ = 9.0
PRIOR_WEIGHT = 64.0
F32 = jnp.float32
BF16 = jnp.bfloat16
NN = (((1,), (0,)), ((), ()))
NT = (((1,), (1,)), ((), ()))
TN = (((0,), (0,)), ((), ()))


def round_up(n, m):
    return -(-n // m) * m


def split3(x):
    hi = x.astype(BF16)
    rest = x - hi.astype(F32)
    mid = rest.astype(BF16)
    low = (rest - mid.astype(F32)).astype(BF16)
    return hi, mid, low


def dot(a, b, dims):
    return lax.dot_general(a, b, dims, preferred_element_type=F32)


def kernel(
    cfg,
    order_ref,
    x_ref,
    dep_ref,
    prec_ref,
    qc_ref,
    bc_ref,
    pc_ref,
    pi_ref,
    mf_ref,
    expand_ref,
    pick_ref,
    prefix_ref,
    co_out,
    io_out,
    co_ref,
    io_ref,
    xs,
    bcs,
    bcr,
    cs,
    cr,
    ts,
    tr,
    beta,
    state,
    work,
    info_out,
    beta_out,
    bc_send,
    bc_recv,
    c_send,
    c_recv,
    t_send,
    t_recv,
    o_send,
    o_recv,
):
    S, O, K, N, NP, T, C, NB, SL, TL = cfg
    sec = lax.axis_index("section")
    ob = lax.axis_index("obs")
    owner = sec < K
    mine = jnp.minimum(sec, K - 1)

    def send(src, dst, send_sem, recv_sem, s, o):
        here = (s == sec) & (o == ob)

        @pl.when(jnp.logical_not(here))
        def _():
            pltpu.make_async_remote_copy(
                src_ref=src,
                dst_ref=dst,
                send_sem=send_sem,
                recv_sem=recv_sem,
                device_id={"section": s, "obs": o},
                device_id_type=pl.DeviceIdType.MESH,
            ).start()

        @pl.when(here)
        def _():
            pltpu.make_async_copy(src, dst, recv_sem).start()

    def sent(src, send_sem, s, o):
        @pl.when(jnp.logical_not((s == sec) & (o == ob)))
        def _():
            pltpu.make_async_copy(src, src, send_sem).wait()

    def got(dst, recv_sem):
        pltpu.make_async_copy(dst, dst, recv_sem).wait()

    def choose(m, load):
        value = load(0)
        for i in range(1, K):
            value = jnp.where(m == i, load(i), value)
        return value

    barrier = pltpu.get_barrier_semaphore()

    def greet(s, _):
        def one(o, _):
            @pl.when(jnp.logical_not((s == sec) & (o == ob)))
            def _():
                pl.semaphore_signal(
                    barrier,
                    inc=1,
                    device_id={"section": s, "obs": o},
                    device_id_type=pl.DeviceIdType.MESH,
                )

            return 0

        return lax.fori_loop(0, O, one, 0)

    lax.fori_loop(0, S, greet, 0)
    for k in range(K):
        line = choose(order_ref[k], lambda i: bc_ref[i : i + 1, :])
        if NB < 128:
            line = jnp.concatenate([line, jnp.full((1, 128 - NB), -1, jnp.int32)], axis=1)
        bcs[k] = jnp.broadcast_to(line, (SL, 128))
    for b in range(NB):
        for i in range(N):
            xs[b, i * K : (i + 1) * K, :] = x_ref[i, :, b * 128 : (b + 1) * 128].astype(F32)
        xs[b, N * K :, :] = jnp.zeros(((NP - N) * K, 128), F32)
    beta[...] = jnp.zeros_like(beta)
    beta[0:N, :] = choose(order_ref[mine], lambda i: pc_ref[:, i, :])

    pl.semaphore_wait(barrier, S * O - 1)


    def send_channels(k, _):
        def one(o, _):
            send(bcs.at[k], bcr.at[sec, ob], bc_send.at[k, o], bc_recv.at[sec, ob], k, o)
            return 0

        return lax.fori_loop(0, O, one, 0)

    lax.fori_loop(0, K, send_channels, 0)

    rows8 = lax.broadcasted_iota(jnp.int32, (O * SL, 128), 0)
    rank_of_row = (rows8 % SL + 1).astype(F32)

    def slots(channel, low):
        inside = (channel >= low) & (channel < low + C)
        rank = dot(jnp.where(inside, 1.0, 0.0).astype(BF16), prefix_ref[...], NN)
        return inside & (rank == rank_of_row)

    @pl.when(owner)
    def _():
        def arrive(w, _):
            def one(o, _):
                got(bcr.at[w, o], bc_recv.at[w, o])
                return 0

            return lax.fori_loop(0, O, one, 0)

        lax.fori_loop(0, S, arrive, 0)

    def row_entry(k, w):
        m = order_ref[k]
        placing = slots(
            jnp.broadcast_to(bcs[k][0:1], (O * SL, 128)), (rows8 // SL) * C
        )
        placing = jnp.where(placing, 1.0, 0.0).astype(BF16)

        def one(o, _):
            got(cr.at[k, o], c_recv.at[k, o])
            return 0

        lax.fori_loop(0, O, one, 0)
        parts = split3(cr[k].reshape(O * SL, 128))
        coef3 = jnp.concatenate(
            [dot(placing, part, TN)[0:NB, 0:NP] for part in parts], axis=0
        ).astype(BF16)
        sub = lax.broadcasted_iota(jnp.int32, (8, 128), 0)
        tiles = [jnp.zeros((8, 128), F32) for _ in range(NB // 8)]
        blocks = []
        for b in range(NB):
            xb = choose(m, lambda i: xs[b, pl.ds(i, NP, stride=K), :])
            xh = xb.astype(BF16)
            blocks.append(xb)
            full = dot(coef3, xh, NN)
            q = b // 8 * 8
            tile = full[q : q + 8] + full[NB + q : NB + q + 8] + full[2 * NB + q : 2 * NB + q + 8]
            tiles[b // 8] = jnp.where(sub == b % 8, tile, tiles[b // 8])
        offset = jnp.concatenate(tiles, axis=0)
        residual = choose(m, lambda i: dep_ref[pl.ds(i, NB, stride=K), :]) - offset
        precision = choose(m, lambda i: prec_ref[pl.ds(i, NB, stride=K), :])
        passed = choose(m, lambda i: qc_ref[pl.ds(i, NB, stride=K), :]).astype(F32)
        weight = passed * precision / (1.0 + precision * residual * residual / HUBER_SQ)
        total = jnp.sum(jnp.sum(weight * residual * residual, axis=0, keepdims=True), axis=1, keepdims=True)
        count = jnp.sum(jnp.sum(passed, axis=0, keepdims=True), axis=1, keepdims=True)
        pieces = [p.astype(F32) for p in split3(residual)]
        line = lax.broadcasted_iota(jnp.int32, (NP, 128), 0)
        grams = []
        for b in range(NB):
            xb = blocks[b]
            left = (weight[b : b + 1] * xb).astype(BF16)
            right = xb
            for p in range(3):
                right = jnp.where(line == N + p, pieces[p][b : b + 1], right)
            grams.append(dot(left, right.astype(BF16), NT))
        gram = jnp.concatenate(grams, axis=0)
        spread = sum(dot(part, expand_ref[...], NN) for part in split3(gram))
        packed = jnp.sum(spread.reshape(NB, NP, TL) * pick_ref[...][None], axis=1)
        out = sum(dot(placing[:, 0:NB], part, NN) for part in split3(packed))
        lane = lax.broadcasted_iota(jnp.int32, (O * SL, TL), 1)
        out = jnp.where(lane == T + N, total, jnp.where(lane == T + N + 1, count, out))
        ts[k] = out.reshape(O, SL, TL)

        def push(o, _):
            send(ts.at[k, o], tr.at[w, ob], t_send.at[k, o], t_recv.at[w, ob], k, o)
            return 0

        lax.fori_loop(0, O, push, 0)

    def owner_slots(w):
        channel = bcr[w].reshape(O * SL, 128)
        low = ob * C
        hit = slots(channel, low)
        value = jnp.sum(jnp.where(hit, (channel - low + 1).astype(F32), 0.0), axis=1, keepdims=True)
        lane = lax.broadcasted_iota(jnp.int32, (O * SL, C), 1).astype(F32)
        return jnp.where(lane == value - 1.0, 1.0, 0.0).astype(BF16)

    def send_info(w):
        send(info_out.at[w], io_ref.at[sec], o_send.at[w, 0], o_recv.at[sec, 0], w, ob)

    def solve(w):
        hot = owner_slots(w)

        @pl.when(w == 0)
        def _():
            state[...] = choose(order_ref[mine], lambda i: pi_ref[:, i, :])

        def one(o, _):
            got(tr.at[w, o], t_recv.at[w, o])
            return 0

        lax.fori_loop(0, O, one, 0)
        terms = tr[w].reshape(O * SL, TL)
        row = lax.broadcasted_iota(jnp.int32, (O * SL, TL), 0)
        sums = jnp.sum(jnp.where(row % SL == 0, terms, 0.0), axis=0, keepdims=True)
        inverse = (sums[:, T + N + 1 : T + N + 2] + PRIOR_WEIGHT) / (sums[:, T + N : T + N + 1] + PRIOR_WEIGHT)
        normal = sum(dot(part, hot, TN) for part in split3(terms)) * inverse

        post = state[...] + normal[0:T]
        work[0:T, :] = post
        work[T:TL, :] = normal[T:TL]
        info_out[w] = post
        state[...] = post * mf_ref[...]

        @pl.when(w == S - 1)
        def _():
            send_info(w)

        cols = []
        for k in range(N):
            at = k * N - k * (k - 1) // 2 - k
            cols.append(work[at : at + NP, :])
        target = work[T : T + NP, :]
        scales, forward, starts = [], [], [0] * N
        for j in range(N):
            scale = lax.rsqrt(cols[j][j - starts[j] : j - starts[j] + 1])
            scales.append(scale)
            base = j // 8 * 8
            factor = cols[j][base - starts[j] :] * scale
            cols[j] = factor
            starts[j] = base
            step = target[j : j + 1] * scale
            forward.append(step)
            target = target - jnp.concatenate([jnp.zeros((base, C), F32), factor * step], axis=0) if base else target - factor * step
            for k in range(j + 1, N):
                kb = k // 8 * 8
                cols[k] = cols[k][kb - starts[k] :] - factor[kb - base :] * factor[k - base : k - base + 1]
                starts[k] = kb
        index = lax.broadcasted_iota(jnp.int32, (NP, C), 0)
        answer = jnp.zeros((NP, C), F32)
        for i in reversed(range(N)):
            base = i // 8 * 8
            dots = jnp.sum(cols[i] * answer[base:], axis=0, keepdims=True)
            value = (forward[i] - dots) * scales[i]
            answer = jnp.where(index == i, value, answer)
        fresh = beta[0:N, :] + answer[0:N]
        beta[0:N, :] = fresh
        beta_out[w] = fresh
        send(beta_out.at[w], co_ref.at[sec], o_send.at[w, 1], o_recv.at[sec, 1], w, ob)

    def window(w, _):
        @pl.when(owner)
        def _():
            hot = owner_slots(w)
            cs[w] = sum(dot(hot, part, NT) for part in split3(beta[...])).reshape(O, SL, 128)

            def one(o, _):
                send(cs.at[w, o], cr.at[sec, ob], c_send.at[w, o], c_recv.at[sec, ob], w, o)
                return 0

            lax.fori_loop(0, O, one, 0)

        @pl.when(sec == w)
        def _():
            def entry(i, _):
                row_entry((w + 1 + i) % K, w)
                return 0

            lax.fori_loop(0, K, entry, 0)

        @pl.when(owner & (w > 0))
        def _():
            send_info(w - 1)

        @pl.when(owner)
        def _():
            solve(w)

        return 0

    lax.fori_loop(0, S, window, 0)

    for k in range(K):
        got(io_ref.at[k], o_recv.at[k, 0])
        io_out[:, k, :] = io_ref[k]
        got(co_ref.at[k], o_recv.at[k, 1])
        co_out[:, k, :] = co_ref[k]

    def drain_rows(k, _):
        def one(o, _):
            sent(bcs.at[k], bc_send.at[k, o], k, o)
            sent(ts.at[k, o], t_send.at[k, o], k, o)
            return 0

        return lax.fori_loop(0, O, one, 0)

    lax.fori_loop(0, K, drain_rows, 0)

    @pl.when(owner)
    def _():
        def drain(w, _):
            def one(o, _):
                sent(cs.at[w, o], c_send.at[w, o], w, o)
                return 0

            lax.fori_loop(0, O, one, 0)
            sent(info_out.at[w], o_send.at[w, 0], w, ob)
            sent(beta_out.at[w], o_send.at[w, 1], w, ob)
            return 0

        lax.fori_loop(0, S, drain, 0)


def local(
    predictors,
    departures,
    obs_precision,
    qc_pass,
    block_channel,
    stream_order,
    prior_coeffs,
    prior_info,
    memory_factor,
):
    S, O = lax.axis_size("section"), lax.axis_size("obs")
    K, N, C = prior_coeffs.shape
    T = prior_info.shape[1]
    NB = block_channel.shape[2]
    R = predictors.shape[3]
    width = R // NB
    assert width == 128 and K <= S and NB <= 128 and NB % 8 == 0
    NP = round_up(N + 3, 8)
    SL = round_up(max(2 * NB // O, 1), 8)
    TL = round_up(T + N + 4, 128)
    pairs = [(i, j) for i in range(N) for j in range(i, N)]
    expand = np.zeros((NP, TL), np.float32)
    pick = np.zeros((NP, TL), np.float32)
    for t, (i, j) in enumerate(pairs):
        expand[j, t] = 1.0
        pick[i, t] = 1.0
    for i in range(N):
        expand[N : N + 3, T + i] = 1.0
        pick[i, T + i] = 1.0
    prefix = (np.arange(128)[:, None] <= np.arange(128)[None, :]).astype(np.float32)
    cfg = (S, O, K, N, NP, T, C, NB, SL, TL)

    def by_block(array):
        return array[0].reshape(K, NB, width).transpose(1, 0, 2).reshape(NB * K, width)

    vm = pl.BlockSpec(memory_space=pltpu.VMEM)
    dma = pltpu.SemaphoreType.DMA
    coeffs, info = pl.pallas_call(
        functools.partial(kernel, cfg),
        out_shape=(
            jax.ShapeDtypeStruct((N, K, C), F32),
            jax.ShapeDtypeStruct((T, K, C), F32),
        ),
        in_specs=[pl.BlockSpec(memory_space=pltpu.SMEM)] + [vm] * 11,
        out_specs=(vm, vm),
        scratch_shapes=[
            pltpu.VMEM((K, N, C), F32),
            pltpu.VMEM((K, T, C), F32),
            pltpu.VMEM((NB, NP * K, 128), F32),
            pltpu.VMEM((K, SL, 128), jnp.int32),
            pltpu.VMEM((S, O, SL, 128), jnp.int32),
            pltpu.VMEM((S, O, SL, 128), F32),
            pltpu.VMEM((K, O, SL, 128), F32),
            pltpu.VMEM((K, O, SL, TL), F32),
            pltpu.VMEM((S, O, SL, TL), F32),
            pltpu.VMEM((128, C), F32),
            pltpu.VMEM((T, C), F32),
            pltpu.VMEM((TL, C), F32),
            pltpu.VMEM((S, T, C), F32),
            pltpu.VMEM((S, N, C), F32),
            dma((K, O)),
            dma((S, O)),
            dma((S, O)),
            dma((K, O)),
            dma((K, O)),
            dma((S, O)),
            dma((S, 2)),
            dma((K, 2)),
        ],
        compiler_params=pltpu.CompilerParams(
            has_side_effects=True, collective_id=0, vmem_limit_bytes=60 * 1024 * 1024
        ),
    )(
        stream_order,
        predictors[0].transpose(1, 0, 2),
        by_block(departures),
        by_block(obs_precision),
        by_block(qc_pass),
        block_channel[0],
        prior_coeffs.transpose(1, 0, 2),
        prior_info.transpose(1, 0, 2),
        memory_factor[None],
        jnp.asarray(expand, BF16),
        jnp.asarray(pick, F32),
        jnp.asarray(prefix, BF16),
    )
    return coeffs.transpose(1, 0, 2)[None], info.transpose(1, 0, 2)[None]


def solution(mesh):
    in_specs = (
        P("section", None, None, "obs"),
        P("section", None, "obs"),
        P("section", None, "obs"),
        P("section", None, "obs"),
        P("section", None, "obs"),
        P(),
        P(None, None, "obs"),
        P(None, None, "obs"),
        P("obs"),
    )
    out_specs = (P("section", None, None, "obs"), P("section", None, None, "obs"))
    return jax.shard_map(local, mesh=mesh, in_specs=in_specs, out_specs=out_specs, check_vma=False)
```

```python
import functools

import jax
import jax.numpy as jnp
import numpy as np
from jax import lax
from jax.experimental import pallas as pl
from jax.experimental.pallas import tpu as pltpu
from jax.sharding import PartitionSpec as P

HUBER_SQ = 9.0
PRIOR_WEIGHT = 64.0
F32 = jnp.float32
BF16 = jnp.bfloat16
NN = (((1,), (0,)), ((), ()))
NT = (((1,), (1,)), ((), ()))
TN = (((0,), (0,)), ((), ()))


def round_up(n, m):
    return -(-n // m) * m


def split3(x):
    hi = x.astype(BF16)
    rest = x - hi.astype(F32)
    mid = rest.astype(BF16)
    low = (rest - mid.astype(F32)).astype(BF16)
    return hi, mid, low


def dot(a, b, dims):
    return lax.dot_general(a, b, dims, preferred_element_type=F32)


def kernel(
    cfg,
    order_ref,
    x_ref,
    dep_ref,
    prec_ref,
    qc_ref,
    bc_ref,
    pc_ref,
    pi_ref,
    mf_ref,
    expand_ref,
    pick_ref,
    prefix_ref,
    co_out,
    io_out,
    co_ref,
    io_ref,
    xs,
    bcs,
    bcr,
    cs,
    cr,
    ts,
    tr,
    beta,
    state,
    work,
    info_out,
    beta_out,
    bc_send,
    bc_recv,
    c_send,
    c_recv,
    t_send,
    t_recv,
    o_send,
    o_recv,
):
    S, O, K, N, NP, T, C, NB, SL, TL = cfg
    sec = lax.axis_index("section")
    ob = lax.axis_index("obs")
    owner = sec < K
    mine = jnp.minimum(sec, K - 1)

    def send(src, dst, send_sem, recv_sem, s, o):
        here = (s == sec) & (o == ob)

        @pl.when(jnp.logical_not(here))
        def _():
            pltpu.make_async_remote_copy(
                src_ref=src,
                dst_ref=dst,
                send_sem=send_sem,
                recv_sem=recv_sem,
                device_id={"section": s, "obs": o},
                device_id_type=pl.DeviceIdType.MESH,
            ).start()

        @pl.when(here)
        def _():
            pltpu.make_async_copy(src, dst, recv_sem).start()

    def sent(src, send_sem, s, o):
        @pl.when(jnp.logical_not((s == sec) & (o == ob)))
        def _():
            pltpu.make_async_copy(src, src, send_sem).wait()

    def got(dst, recv_sem):
        pltpu.make_async_copy(dst, dst, recv_sem).wait()

    def choose(m, load):
        value = load(0)
        for i in range(1, K):
            value = jnp.where(m == i, load(i), value)
        return value

    barrier = pltpu.get_barrier_semaphore()

    def greet(s, _):
        def one(o, _):
            @pl.when(jnp.logical_not((s == sec) & (o == ob)))
            def _():
                pl.semaphore_signal(
                    barrier,
                    inc=1,
                    device_id={"section": s, "obs": o},
                    device_id_type=pl.DeviceIdType.MESH,
                )

            return 0

        return lax.fori_loop(0, O, one, 0, unroll=8 if O % 8 == 0 else 1)

    lax.fori_loop(0, S, greet, 0)
    for k in range(K):
        line = choose(order_ref[k], lambda i: bc_ref[i : i + 1, :])
        if NB < 128:
            line = jnp.concatenate([line, jnp.full((1, 128 - NB), -1, jnp.int32)], axis=1)
        bcs[k] = jnp.broadcast_to(line, (SL, 128))
    for b in range(NB):
        for i in range(N):
            xs[b, i * K : (i + 1) * K, :] = x_ref[i, :, b * 128 : (b + 1) * 128].astype(F32)
        xs[b, N * K :, :] = jnp.zeros(((NP - N) * K, 128), F32)
    beta[...] = jnp.zeros_like(beta)
    beta[0:N, :] = choose(order_ref[mine], lambda i: pc_ref[:, i, :])

    pl.semaphore_wait(barrier, S * O - 1)


    def send_channels(k, _):
        def one(o, _):
            send(bcs.at[k], bcr.at[sec, ob], bc_send.at[k, o], bc_recv.at[sec, ob], k, o)
            return 0

        return lax.fori_loop(0, O, one, 0, unroll=8 if O % 8 == 0 else 1)

    lax.fori_loop(0, K, send_channels, 0)

    rows8 = lax.broadcasted_iota(jnp.int32, (O * SL, 128), 0)
    rank_of_row = (rows8 % SL + 1).astype(F32)

    def slots(channel, low):
        inside = (channel >= low) & (channel < low + C)
        rank = dot(jnp.where(inside, 1.0, 0.0).astype(BF16), prefix_ref[...], NN)
        return inside & (rank == rank_of_row)

    @pl.when(owner)
    def _():
        def arrive(w, _):
            def one(o, _):
                got(bcr.at[w, o], bc_recv.at[w, o])
                return 0

            return lax.fori_loop(0, O, one, 0, unroll=8 if O % 8 == 0 else 1)

        lax.fori_loop(0, S, arrive, 0)

    def row_entry(k, w):
        m = order_ref[k]
        placing = slots(
            jnp.broadcast_to(bcs[k][0:1], (O * SL, 128)), (rows8 // SL) * C
        )
        placing = jnp.where(placing, 1.0, 0.0).astype(BF16)

        def one(o, _):
            got(cr.at[k, o], c_recv.at[k, o])
            return 0

        lax.fori_loop(0, O, one, 0, unroll=8 if O % 8 == 0 else 1)
        parts = split3(cr[k].reshape(O * SL, 128))
        coef3 = jnp.concatenate(
            [dot(placing, part, TN)[0:NB, 0:NP] for part in parts], axis=0
        ).astype(BF16)
        sub = lax.broadcasted_iota(jnp.int32, (8, 128), 0)
        tiles = [jnp.zeros((8, 128), F32) for _ in range(NB // 8)]
        blocks = []
        for b in range(NB):
            xb = choose(m, lambda i: xs[b, pl.ds(i, NP, stride=K), :])
            xh = xb.astype(BF16)
            blocks.append(xb)
            full = dot(coef3, xh, NN)
            q = b // 8 * 8
            tile = full[q : q + 8] + full[NB + q : NB + q + 8] + full[2 * NB + q : 2 * NB + q + 8]
            tiles[b // 8] = jnp.where(sub == b % 8, tile, tiles[b // 8])
        offset = jnp.concatenate(tiles, axis=0)
        residual = choose(m, lambda i: dep_ref[pl.ds(i, NB, stride=K), :]) - offset
        precision = choose(m, lambda i: prec_ref[pl.ds(i, NB, stride=K), :])
        passed = choose(m, lambda i: qc_ref[pl.ds(i, NB, stride=K), :]).astype(F32)
        weight = passed * precision / (1.0 + precision * residual * residual / HUBER_SQ)
        total = jnp.sum(jnp.sum(weight * residual * residual, axis=0, keepdims=True), axis=1, keepdims=True)
        count = jnp.sum(jnp.sum(passed, axis=0, keepdims=True), axis=1, keepdims=True)
        pieces = [p.astype(F32) for p in split3(residual)]
        line = lax.broadcasted_iota(jnp.int32, (NP, 128), 0)
        grams = []
        for b in range(NB):
            xb = blocks[b]
            left = (weight[b : b + 1] * xb).astype(BF16)
            right = xb
            for p in range(3):
                right = jnp.where(line == N + p, pieces[p][b : b + 1], right)
            grams.append(dot(left, right.astype(BF16), NT))
        gram = jnp.concatenate(grams, axis=0)
        spread = sum(dot(part, expand_ref[...], NN) for part in split3(gram))
        packed = jnp.sum(spread.reshape(NB, NP, TL) * pick_ref[...][None], axis=1)
        out = sum(dot(placing[:, 0:NB], part, NN) for part in split3(packed))
        lane = lax.broadcasted_iota(jnp.int32, (O * SL, TL), 1)
        out = jnp.where(lane == T + N, total, jnp.where(lane == T + N + 1, count, out))
        ts[k] = out.reshape(O, SL, TL)

        def push(o, _):
            send(ts.at[k, o], tr.at[w, ob], t_send.at[k, o], t_recv.at[w, ob], k, o)
            return 0

        lax.fori_loop(0, O, push, 0, unroll=8 if O % 8 == 0 else 1)

    def owner_slots(w):
        channel = bcr[w].reshape(O * SL, 128)
        low = ob * C
        hit = slots(channel, low)
        value = jnp.sum(jnp.where(hit, (channel - low + 1).astype(F32), 0.0), axis=1, keepdims=True)
        lane = lax.broadcasted_iota(jnp.int32, (O * SL, C), 1).astype(F32)
        return jnp.where(lane == value - 1.0, 1.0, 0.0).astype(BF16)

    def send_info(w):
        send(info_out.at[w], io_ref.at[sec], o_send.at[w, 0], o_recv.at[sec, 0], w, ob)

    def solve(w):
        hot = owner_slots(w)

        @pl.when(w == 0)
        def _():
            state[...] = choose(order_ref[mine], lambda i: pi_ref[:, i, :])

        def one(o, _):
            got(tr.at[w, o], t_recv.at[w, o])
            return 0

        lax.fori_loop(0, O, one, 0, unroll=8 if O % 8 == 0 else 1)
        terms = tr[w].reshape(O * SL, TL)
        row = lax.broadcasted_iota(jnp.int32, (O * SL, TL), 0)
        sums = jnp.sum(jnp.where(row % SL == 0, terms, 0.0), axis=0, keepdims=True)
        inverse = (sums[:, T + N + 1 : T + N + 2] + PRIOR_WEIGHT) / (sums[:, T + N : T + N + 1] + PRIOR_WEIGHT)
        normal = sum(dot(part, hot, TN) for part in split3(terms)) * inverse

        post = state[...] + normal[0:T]
        work[0:T, :] = post
        work[T:TL, :] = normal[T:TL]
        info_out[w] = post
        state[...] = post * mf_ref[...]

        @pl.when(w == S - 1)
        def _():
            send_info(w)

        cols = []
        for k in range(N):
            at = k * N - k * (k - 1) // 2 - k
            cols.append(work[at : at + NP, :])
        target = work[T : T + NP, :]
        scales, forward, starts = [], [], [0] * N
        for j in range(N):
            scale = lax.rsqrt(cols[j][j - starts[j] : j - starts[j] + 1])
            scales.append(scale)
            base = j // 8 * 8
            factor = cols[j][base - starts[j] :] * scale
            cols[j] = factor
            starts[j] = base
            step = target[j : j + 1] * scale
            forward.append(step)
            target = target - jnp.concatenate([jnp.zeros((base, C), F32), factor * step], axis=0) if base else target - factor * step
            for k in range(j + 1, N):
                kb = k // 8 * 8
                cols[k] = cols[k][kb - starts[k] :] - factor[kb - base :] * factor[k - base : k - base + 1]
                starts[k] = kb
        index = lax.broadcasted_iota(jnp.int32, (NP, C), 0)
        answer = jnp.zeros((NP, C), F32)
        for i in reversed(range(N)):
            base = i // 8 * 8
            dots = jnp.sum(cols[i] * answer[base:], axis=0, keepdims=True)
            value = (forward[i] - dots) * scales[i]
            answer = jnp.where(index == i, value, answer)
        fresh = beta[0:N, :] + answer[0:N]
        beta[0:N, :] = fresh
        beta_out[w] = fresh
        send(beta_out.at[w], co_ref.at[sec], o_send.at[w, 1], o_recv.at[sec, 1], w, ob)

    def window(w, _):
        @pl.when(owner)
        def _():
            hot = owner_slots(w)
            cs[w] = sum(dot(hot, part, NT) for part in split3(beta[...])).reshape(O, SL, 128)

            def one(o, _):
                send(cs.at[w, o], cr.at[sec, ob], c_send.at[w, o], c_recv.at[sec, ob], w, o)
                return 0

            lax.fori_loop(0, O, one, 0, unroll=8 if O % 8 == 0 else 1)

        @pl.when(sec == w)
        def _():
            def entry(i, _):
                row_entry((w + 1 + i) % K, w)
                return 0

            lax.fori_loop(0, K, entry, 0)

        @pl.when(owner & (w > 0))
        def _():
            send_info(w - 1)

        @pl.when(owner)
        def _():
            solve(w)

        return 0

    lax.fori_loop(0, S, window, 0)

    for k in range(K):
        got(io_ref.at[k], o_recv.at[k, 0])
        io_out[:, k, :] = io_ref[k]
        got(co_ref.at[k], o_recv.at[k, 1])
        co_out[:, k, :] = co_ref[k]

    def drain_rows(k, _):
        def one(o, _):
            sent(bcs.at[k], bc_send.at[k, o], k, o)
            sent(ts.at[k, o], t_send.at[k, o], k, o)
            return 0

        return lax.fori_loop(0, O, one, 0, unroll=8 if O % 8 == 0 else 1)

    lax.fori_loop(0, K, drain_rows, 0)

    @pl.when(owner)
    def _():
        def drain(w, _):
            def one(o, _):
                sent(cs.at[w, o], c_send.at[w, o], w, o)
                return 0

            lax.fori_loop(0, O, one, 0, unroll=8 if O % 8 == 0 else 1)
            sent(info_out.at[w], o_send.at[w, 0], w, ob)
            sent(beta_out.at[w], o_send.at[w, 1], w, ob)
            return 0

        lax.fori_loop(0, S, drain, 0)


def local(
    predictors,
    departures,
    obs_precision,
    qc_pass,
    block_channel,
    stream_order,
    prior_coeffs,
    prior_info,
    memory_factor,
):
    S, O = lax.axis_size("section"), lax.axis_size("obs")
    K, N, C = prior_coeffs.shape
    T = prior_info.shape[1]
    NB = block_channel.shape[2]
    R = predictors.shape[3]
    width = R // NB
    assert width == 128 and K <= S and NB <= 128 and NB % 8 == 0
    NP = round_up(N + 3, 8)
    SL = round_up(max(2 * NB // O, 1), 8)
    TL = round_up(T + N + 4, 128)
    pairs = [(i, j) for i in range(N) for j in range(i, N)]
    expand = np.zeros((NP, TL), np.float32)
    pick = np.zeros((NP, TL), np.float32)
    for t, (i, j) in enumerate(pairs):
        expand[j, t] = 1.0
        pick[i, t] = 1.0
    for i in range(N):
        expand[N : N + 3, T + i] = 1.0
        pick[i, T + i] = 1.0
    prefix = (np.arange(128)[:, None] <= np.arange(128)[None, :]).astype(np.float32)
    cfg = (S, O, K, N, NP, T, C, NB, SL, TL)

    def by_block(array):
        return array[0].reshape(K, NB, width).transpose(1, 0, 2).reshape(NB * K, width)

    vm = pl.BlockSpec(memory_space=pltpu.VMEM)
    dma = pltpu.SemaphoreType.DMA
    coeffs, info = pl.pallas_call(
        functools.partial(kernel, cfg),
        out_shape=(
            jax.ShapeDtypeStruct((N, K, C), F32),
            jax.ShapeDtypeStruct((T, K, C), F32),
        ),
        in_specs=[pl.BlockSpec(memory_space=pltpu.SMEM)] + [vm] * 11,
        out_specs=(vm, vm),
        scratch_shapes=[
            pltpu.VMEM((K, N, C), F32),
            pltpu.VMEM((K, T, C), F32),
            pltpu.VMEM((NB, NP * K, 128), F32),
            pltpu.VMEM((K, SL, 128), jnp.int32),
            pltpu.VMEM((S, O, SL, 128), jnp.int32),
            pltpu.VMEM((S, O, SL, 128), F32),
            pltpu.VMEM((K, O, SL, 128), F32),
            pltpu.VMEM((K, O, SL, TL), F32),
            pltpu.VMEM((S, O, SL, TL), F32),
            pltpu.VMEM((128, C), F32),
            pltpu.VMEM((T, C), F32),
            pltpu.VMEM((TL, C), F32),
            pltpu.VMEM((S, T, C), F32),
            pltpu.VMEM((S, N, C), F32),
            dma((K, O)),
            dma((S, O)),
            dma((S, O)),
            dma((K, O)),
            dma((K, O)),
            dma((S, O)),
            dma((S, 2)),
            dma((K, 2)),
        ],
        compiler_params=pltpu.CompilerParams(
            has_side_effects=True, collective_id=0, vmem_limit_bytes=60 * 1024 * 1024
        ),
    )(
        stream_order,
        predictors[0].transpose(1, 0, 2),
        by_block(departures),
        by_block(obs_precision),
        by_block(qc_pass),
        block_channel[0],
        prior_coeffs.transpose(1, 0, 2),
        prior_info.transpose(1, 0, 2),
        memory_factor[None],
        jnp.asarray(expand, BF16),
        jnp.asarray(pick, F32),
        jnp.asarray(prefix, BF16),
    )
    return coeffs.transpose(1, 0, 2)[None], info.transpose(1, 0, 2)[None]


def solution(mesh):
    in_specs = (
        P("section", None, None, "obs"),
        P("section", None, "obs"),
        P("section", None, "obs"),
        P("section", None, "obs"),
        P("section", None, "obs"),
        P(),
        P(None, None, "obs"),
        P(None, None, "obs"),
        P("obs"),
    )
    out_specs = (P("section", None, None, "obs"), P("section", None, None, "obs"))
    return jax.shard_map(local, mesh=mesh, in_specs=in_specs, out_specs=out_specs, check_vma=False)
```
